32 devices in a mesh: ctx: 8 (over z, x), head: 4 (over y, core).
Axes of the slice: x: 2, y: 2, z: 4, core: 2. Of those that a mesh axis runs over, the one named last changes fastest.
Arguments:
- query: bfloat16 [4096, 16, 128], P('ctx', 'head'), may hold values from -24 to 24
- key: bfloat16 [4096, 16, 128], P('ctx', 'head'), may hold values from -6 to 6
- value: bfloat16 [4096, 16, 128], P('ctx', 'head'), may hold values from -6 to 6
- out_grad: bfloat16 [4096, 16, 128], P('ctx', 'head'), may hold values from -6 to 6
- random_links: int32 [64, 16, 3], P(None, 'head'), may hold values from 0 to 63, as said below
Outputs:
- attended: bfloat16 [4096, 16, 128], P('ctx', 'head')
- query_grad: bfloat16 [4096, 16, 128], P('ctx', 'head')
- key_grad: bfloat16 [4096, 16, 128], P('ctx', 'head')
- value_grad: bfloat16 [4096, 16, 128], P('ctx', 'head')
The draws below stay inside these ranges and needn't reach their ends.
Inputs may be any that keep to these rules, and one draw needn't show every extreme that they name: `random_links`: within one head, the 24 random entries of the query blocks o * 8 to o * 8 + 7 name blocks of any one run p * 8 to p * 8 + 7 at most 4 times, and for each such run of query blocks and head some run p is named exactly 4 times.
All inputs are finite; a program needn't handle non-finite values.
Results may differ from the reference program's by a relative error of at most 0.012.
Values may be sent and summed in bfloat16 or wider, within the bound.
No kernel may reach another device: no remote copies, remote signals or barrier semaphores. Data moves between devices by JAX's collectives and lax.ppermute only.
A program may use at most 128 MiB of HBM per device.

```python
import math
import jax
import jax.numpy as jnp
from jax import lax

BLOCK = 64
HD = 128
R = 3
HEADS = 16
BPD = 8
NB = 64
SEQ = 4096
CAP = 4
N_CTX = 8


def draw_query(key, part):
    base_key = jax.random.fold_in(key, 21)
    drawn = jnp.clip(jax.random.normal(base_key, (SEQ, HEADS, HD), jnp.float32), -6.0, 6.0)
    return drawn.astype(jnp.bfloat16)


def draw_key(key, part):
    base_key = jax.random.fold_in(key, 22)
    drawn = jnp.clip(jax.random.normal(base_key, (SEQ, HEADS, HD), jnp.float32), -6.0, 6.0)
    return drawn.astype(jnp.bfloat16)


def one_table(table_key):
    slot_count = N_CTX * CAP
    ref_count = BPD * R
    first_key, second_key, third_key, fourth_key = jax.random.split(table_key, 4)
    shuffled = jax.random.permutation(first_key, slot_count)
    priority = jnp.zeros((slot_count,), jnp.int32).at[shuffled].set(jnp.arange(slot_count, dtype=jnp.int32))
    favored = jax.random.randint(second_key, (), 0, N_CTX)
    priority = jnp.where(jnp.arange(slot_count, dtype=jnp.int32) // CAP == favored, -1, priority)
    picked = jnp.argsort(priority, stable=True)[:ref_count]
    holders = (picked // CAP)[jax.random.permutation(third_key, ref_count)]
    within = jax.random.randint(fourth_key, (ref_count,), 0, BPD)
    return (holders * BPD + within).astype(jnp.int32)


def draw_random_links(key, part):
    table_keys = jax.random.split(jax.random.fold_in(key, 31), N_CTX * HEADS)
    tables = jax.vmap(one_table)(table_keys)
    return tables.reshape(N_CTX, HEADS, BPD, R).transpose(0, 2, 1, 3).reshape(NB, HEADS, R)


def steps_of(own_key, shape, pieces, least, top_value):
    gain, own = 1.0, jax.random.fold_in(own_key, 6)
    for position, shards_of in pieces:
        heights = jnp.exp(jax.random.uniform(jax.random.fold_in(own, position), (shards_of,), jnp.float32, least / len(pieces), top_value / len(pieces)))
        gain = gain * jnp.repeat(heights, shape[position] // shards_of).reshape([-1 if axis == position else 1 for axis in range(len(shape))])
    return gain


def scatter_about(stream_key, dims, spread, reach, cuts=(), kind=jnp.bfloat16):
    values = jax.random.normal(stream_key, dims, jnp.float32) * spread
    if len(cuts) > 0:
        values = steps_of(stream_key, dims, cuts, -0.22, 0.18) * values
    return jnp.clip(values, min=-reach, max=reach).astype(kind)


def setup_inputs(seed: int = 0) -> dict:
    key_list = jax.random.split(jax.random.key(seed), 6)
    return {
        "query": draw_query(jax.random.fold_in(key_list[5], 71), 0),
        "key": draw_key(jax.random.fold_in(key_list[5], 71), 0),
        "value": scatter_about(key_list[2], (SEQ, HEADS, HD), 1.0, 6.0, ((0, 8), (1, 4))),
        "out_grad": scatter_about(key_list[3], (SEQ, HEADS, HD), 1.0, 6.0, ((0, 8), (1, 4))),
        "random_links": draw_random_links(jax.random.fold_in(key_list[5], 71), 0),
    }


def to_low(array):
    return lax.optimization_barrier(array.astype(jnp.bfloat16)).astype(jnp.float32)

def take_blocks(table_one, index_one):
    return table_one[index_one]

def add_blocks(total_one, index_one, terms_one):
    return total_one.at[index_one].add(terms_one)

def reference(query, key, value, out_grad, random_links):
    scaling = 1.0 / math.sqrt(HD)
    kind_count = 5 + R

    def head_major(array):
        return array.reshape(NB, BLOCK, HEADS, HD).transpose(2, 0, 1, 3)
    query_all = head_major(query)
    key_all = head_major(key)
    value_all = head_major(value)
    grad_all = head_major(out_grad)
    block_ids = jnp.arange(NB, dtype=jnp.int32)
    previous = jnp.maximum(block_ids - 1, 0)
    following = jnp.minimum(block_ids + 1, NB - 1)
    fixed_ids = jnp.stack((previous, block_ids, following, jnp.zeros_like(block_ids), jnp.full_like(block_ids, NB - 1)), axis=1)
    key_lists = jnp.concatenate((jnp.broadcast_to(fixed_ids[:, None, :], (NB, HEADS, 5)), random_links.astype(jnp.int32)), axis=2)
    usable = jnp.concatenate(((block_ids > 0)[:, None], jnp.ones((NB, 1), bool), (block_ids < NB - 1)[:, None], jnp.ones((NB, kind_count - 3), bool)), axis=1)
    col_valid = jnp.repeat(usable, BLOCK, axis=1)
    far_entry = (jnp.arange(kind_count) >= 5)[None, None, :, None, None]

    def advance(carried, group):
        key_total, value_total = carried
        start = (group * BPD).astype(jnp.int32)
        query_group = lax.dynamic_slice_in_dim(query_all, start, BPD, 1).astype(jnp.float32)
        grad_group = lax.dynamic_slice_in_dim(grad_all, start, BPD, 1).astype(jnp.float32)
        list_group = lax.dynamic_slice_in_dim(key_lists, start, BPD, 0).transpose(1, 0, 2)
        valid_group = lax.dynamic_slice_in_dim(col_valid, start, BPD, 0)
        key_group = jax.vmap(take_blocks)(key_all, list_group).reshape(HEADS, BPD, kind_count * BLOCK, HD).astype(jnp.float32)
        value_group = jax.vmap(take_blocks)(value_all, list_group).reshape(HEADS, BPD, kind_count * BLOCK, HD).astype(jnp.float32)
        scores = jnp.einsum('hgbd,hgkd->hgbk', query_group, key_group) * scaling
        valid_mask = valid_group[None, :, None, :]
        scores = jnp.where(valid_mask, scores, -1e+30)
        row_max = lax.optimization_barrier(jnp.max(scores, axis=-1, keepdims=True))
        powers = jnp.where(valid_mask, jnp.exp(scores - row_max), 0.0)
        probs = powers / lax.optimization_barrier(jnp.sum(powers, axis=-1, keepdims=True))
        probs_low = to_low(probs)
        attended = jnp.einsum('hgbk,hgkd->hgbd', probs_low, value_group).astype(jnp.bfloat16)
        row_delta = lax.optimization_barrier(jnp.sum(grad_group * attended.astype(jnp.float32), axis=-1))
        grad_probs = jnp.einsum('hgbd,hgkd->hgbk', grad_group, value_group)
        grad_scores = to_low(probs * (grad_probs - row_delta[..., None]))
        query_part = (scaling * jnp.einsum('hgbk,hgkd->hgbd', grad_scores, key_group)).astype(jnp.bfloat16)
        key_terms = scaling * jnp.einsum('hgbk,hgbd->hgkd', grad_scores, query_group)
        value_terms = jnp.einsum('hgbk,hgbd->hgkd', probs_low, grad_group)
        key_terms = key_terms.reshape(HEADS, BPD, kind_count, BLOCK, HD)
        value_terms = value_terms.reshape(HEADS, BPD, kind_count, BLOCK, HD)
        key_terms = jnp.where(far_entry, to_low(key_terms), key_terms)
        value_terms = jnp.where(far_entry, to_low(value_terms), value_terms)
        flat_ids = list_group.reshape(HEADS, BPD * kind_count)
        key_total = jax.vmap(add_blocks)(key_total, flat_ids, key_terms.reshape(HEADS, BPD * kind_count, BLOCK, HD))
        value_total = jax.vmap(add_blocks)(value_total, flat_ids, value_terms.reshape(HEADS, BPD * kind_count, BLOCK, HD))
        return ((key_total, value_total), (attended, query_part))
    zeros_start = jnp.zeros((HEADS, NB, BLOCK, HD), jnp.float32)
    (key_total, value_total), (attended, query_part) = lax.scan(advance, (zeros_start, zeros_start), jnp.arange(NB // BPD, dtype=jnp.int32))

    def seq_from_groups(array):
        return array.transpose(0, 2, 3, 1, 4).reshape(SEQ, HEADS, HD)

    def seq_from_heads(array):
        return array.transpose(1, 2, 0, 3).reshape(SEQ, HEADS, HD)
    return (seq_from_groups(attended), seq_from_groups(query_part), seq_from_heads(key_total).astype(jnp.bfloat16), seq_from_heads(value_total).astype(jnp.bfloat16))
```

```python
import functools
import math

import jax
import jax.numpy as jnp
from jax import lax
from jax.experimental import pallas as pl
from jax.experimental.pallas import tpu as pltpu
from jax.sharding import PartitionSpec as P

BLOCK = 64
CHUNKS = 1
F32 = jnp.float32
BF16 = jnp.bfloat16


def dot(a, b, dims):
    return lax.dot_general(a, b, (dims, ((), ())), preferred_element_type=F32)


def serve_kernel(wanted_ref, k_ref, v_ref, out_ref, *, head0, slots, capacity):
    h = head0 + pl.program_id(0)

    def body(s, carry):
        j = jnp.maximum(wanted_ref[h * slots + s], 0)
        t = s // capacity
        c = s - t * capacity
        out_ref[t, 0, c, 0] = k_ref[0, j]
        out_ref[t, 0, c, 1] = v_ref[0, j]
        return carry

    lax.fori_loop(0, slots, body, 0, unroll=4)


def attend_kernel(
    place_ref,
    flag_ref,
    q_ref,
    g_ref,
    k_ref,
    v_ref,
    prev_ref,
    next_ref,
    anchor_ref,
    arr_ref,
    att_ref,
    dq_ref,
    near_ref,
    edge_ref,
    dan_ref,
    send_ref,
    kx,
    vx,
    kc,
    vc,
    accw,
    acca,
    *,
    head0,
    per_device,
    links,
    capacity,
    scaling,
):
    h = head0 + pl.program_id(0)
    hd = q_ref.shape[-1]
    refs = per_device * links
    wide = 3 * BLOCK
    fixed = 5 * BLOCK
    total = fixed + links * BLOCK
    for dst, src, side in ((kx, k_ref, 0), (vx, v_ref, 1)):
        dst[0] = prev_ref[0, side]
        dst[1 : per_device + 1] = src[0]
        dst[per_device + 1] = next_ref[0, side]
    for dst, side in ((kc, 0), (vc, 1)):
        for slot in range(2):
            dst[slot, wide:fixed] = anchor_ref[0, :, side].reshape(2 * BLOCK, hd)
    accw[...] = jnp.zeros_like(accw)
    acca[...] = jnp.zeros_like(acca)
    no_prev = flag_ref[0] == 0
    no_next = flag_ref[1] == 0

    def one(i, slot):
        places = [place_ref[h * refs + i * links + r] for r in range(links)]
        for dst, src, side in ((kc, kx, 0), (vc, vx, 1)):
            dst[slot, 0:wide] = src[pl.ds(i, 3)].reshape(wide, hd)
            for r in range(links):
                t = places[r] // capacity
                c = places[r] - t * capacity
                dst[slot, fixed + r * BLOCK : fixed + (r + 1) * BLOCK] = arr_ref[t, 0, c, side]
        q = q_ref[0, i]
        g = g_ref[0, i]
        keys = kc[slot]
        vals = vc[slot]
        s = dot(q, keys, ((1,), (1,)))
        dp = dot(g, vals, ((1,), (1,)))
        col = lax.broadcasted_iota(jnp.int32, (BLOCK, total), 1)
        low = jnp.where(jnp.logical_and(i == 0, no_prev), BLOCK, 0)
        high = jnp.where(jnp.logical_and(i == per_device - 1, no_next), 2 * BLOCK, wide)
        hidden = (col < low) | ((col >= high) & (col < wide))
        s = jnp.where(hidden, -1e30, s)
        m = jnp.max(s, axis=1, keepdims=True)
        p = jnp.where(hidden, 0.0, jnp.exp((s - m) * scaling))
        p = p * (1.0 / jnp.sum(p, axis=1, keepdims=True))
        low_p = p.astype(BF16)
        o = dot(low_p, vals, ((1,), (0,))).astype(BF16)
        att_ref[0, i] = o
        delta = jnp.sum(g.astype(F32) * o.astype(F32), axis=1, keepdims=True)
        ds = (p * (dp - delta)).astype(BF16)
        dq_ref[0, i] = (scaling * dot(ds, keys, ((1,), (0,)))).astype(BF16)
        dk = scaling * dot(ds, q, ((0,), (0,)))
        dv = dot(low_p, g, ((0,), (0,)))
        for side, term in ((0, dk), (1, dv)):
            accw[side, pl.ds(i, 3)] += term[:wide].reshape(3, BLOCK, hd)
            acca[side] += term[wide:fixed].reshape(2, BLOCK, hd)
            for r in range(links):
                t = places[r] // capacity
                c = places[r] - t * capacity
                send_ref[t, 0, c, side] = term[
                    fixed + r * BLOCK : fixed + (r + 1) * BLOCK
                ].astype(BF16)

    def pair(n, carry):
        one(2 * n, 0)
        one(2 * n + 1, 1)
        return carry

    lax.fori_loop(0, per_device // 2, pair, 0)
    near_ref[0] = accw[:, 1 : per_device + 1]
    edge_ref[0, 0] = accw[:, 0].astype(BF16)
    edge_ref[0, 1] = accw[:, per_device + 1].astype(BF16)
    dan_ref[0, 0] = acca[:, 0]
    dan_ref[0, 1] = acca[:, 1]


def finish_kernel(
    wanted_ref, flag_ref, near_ref, back_ref, up_ref, down_ref, anchor_ref, dk_ref, dv_ref, acc,
    *, head0, slots, capacity, per_device,
):
    h = head0 + pl.program_id(0)
    acc[...] = near_ref[0]
    acc[:, 0] += up_ref[0].astype(F32)
    acc[:, per_device - 1] += down_ref[0].astype(F32)

    @pl.when(flag_ref[0] == 0)
    def _():
        acc[:, 0] += anchor_ref[0]

    @pl.when(flag_ref[1] == 0)
    def _():
        acc[:, per_device - 1] += anchor_ref[0]

    def body(s, carry):
        j = wanted_ref[h * slots + s]
        t = s // capacity
        c = s - t * capacity

        @pl.when(j >= 0)
        def _():
            acc[:, j] += back_ref[t, 0, c].astype(F32)

        return carry

    lax.fori_loop(0, slots, body, 0)
    dk_ref[0] = acc[0].astype(BF16)
    dv_ref[0] = acc[1].astype(BF16)


def local(query, key, value, out_grad, random_links):
    seq_local, heads, hd = query.shape
    per_device = seq_local // BLOCK
    links = random_links.shape[2]
    ctx = lax.axis_size("ctx")
    me = lax.axis_index("ctx")
    refs = per_device * links
    capacity = max(2, (5 * refs + 4 * ctx - 1) // (4 * ctx))
    slots = ctx * capacity
    scaling = 1.0 / math.sqrt(hd)
    chunks = CHUNKS if heads % CHUNKS == 0 else 1
    hc = heads // chunks

    def head_major(array):
        return array.reshape(per_device, BLOCK, heads, hd).transpose(2, 0, 1, 3)

    def seq_major(array):
        return array.transpose(1, 2, 0, 3).reshape(seq_local, heads, hd)

    k = head_major(key)
    v = head_major(value)
    q = head_major(query)
    g = head_major(out_grad)

    table = random_links.transpose(1, 0, 2).reshape(heads, ctx, refs)
    aimed = (table // per_device) == me
    before = jnp.arange(refs)[:, None] > jnp.arange(refs)[None, :]
    order = jnp.sum((aimed[:, :, None, :] & before).astype(jnp.int32), axis=3)
    hit = aimed[:, :, None, :] & (order[:, :, None, :] == jnp.arange(capacity)[:, None])
    wanted = jnp.sum(jnp.where(hit, table[:, :, None, :] % per_device + 1, 0), axis=3) - 1
    wanted = wanted.reshape(heads * slots)
    own = lax.dynamic_index_in_dim(table, me, 1, keepdims=False)
    owner = own // per_device
    same = (owner[:, :, None] == owner[:, None, :]) & before
    place = owner * capacity + jnp.sum(same.astype(jnp.int32), axis=2)
    place = place.reshape(heads * refs)
    flags = jnp.stack((me > 0, me < ctx - 1)).astype(jnp.int32)

    def smem():
        return pl.BlockSpec(memory_space=pltpu.SMEM)

    def head_block(shape, head0):
        zeros = (0,) * (len(shape))
        return pl.BlockSpec((1,) + shape, lambda n: (head0 + n,) + zeros)

    def slot_block():
        return pl.BlockSpec(
            (ctx, 1, capacity, 2, BLOCK, hd), lambda n: (0, n, 0, 0, 0, 0)
        )

    blk = (per_device, BLOCK, hd)
    slot_shape = jax.ShapeDtypeStruct((ctx, hc, capacity, 2, BLOCK, hd), BF16)

    def params(limit=None):
        return pltpu.CompilerParams(
            dimension_semantics=("arbitrary",), vmem_limit_bytes=limit
        )

    def serve(c):
        return pl.pallas_call(
            functools.partial(
                serve_kernel, head0=c * hc, slots=slots, capacity=capacity
            ),
            grid=(hc,),
            in_specs=[smem(), head_block(blk, c * hc), head_block(blk, c * hc)],
            out_specs=slot_block(),
            out_shape=slot_shape,
            compiler_params=params(),
            cost_estimate=pl.CostEstimate(
                flops=0, bytes_accessed=4 * hc * slots * BLOCK * hd * 2, transcendentals=0
            ),
            name="serve",
        )(wanted, k, v)

    def exchange(array):
        return lax.all_to_all(array, "ctx", split_axis=0, concat_axis=0, tiled=True)

    arrived = [exchange(serve(c)) for c in range(chunks)]

    kv = jnp.stack((k, v), axis=1)
    first, last = kv[:, :, 0], kv[:, :, per_device - 1]
    up = [(n, n + 1) for n in range(ctx - 1)]
    down = [(n + 1, n) for n in range(ctx - 1)]
    prev_edge = lax.ppermute(last, "ctx", up)
    next_edge = lax.ppermute(first, "ctx", down)

    bits = [1 << b for b in range(ctx.bit_length() - 1)]
    half = bits[-1]
    swap = [(n, n ^ half) for n in range(ctx)]
    lower = me < half
    anchor = jnp.where(lower, first, last)
    spread = []
    known = 1
    for bit in bits[:-1]:
        pairs = [(n, n + bit) for n in range(known)]
        pairs += [(ctx - 1 - a, ctx - 1 - b) for a, b in pairs]
        spread.append((bit, pairs))
        moved = lax.ppermute(anchor, "ctx", pairs)
        rank = jnp.where(lower, me, ctx - 1 - me)
        anchor = jnp.where((rank >= known) & (rank < 2 * known), moved, anchor)
        known *= 2
    other = lax.ppermute(anchor, "ctx", swap)
    anchors = jnp.stack(
        (jnp.where(lower, anchor, other), jnp.where(lower, other, anchor)), axis=1
    )

    def attend(c):
        h0 = c * hc
        return pl.pallas_call(
            functools.partial(
                attend_kernel,
                head0=h0,
                per_device=per_device,
                links=links,
                capacity=capacity,
                scaling=scaling,
            ),
            grid=(hc,),
            in_specs=[
                smem(),
                smem(),
                head_block(blk, h0),
                head_block(blk, h0),
                head_block(blk, h0),
                head_block(blk, h0),
                head_block((2, BLOCK, hd), h0),
                head_block((2, BLOCK, hd), h0),
                head_block((2, 2, BLOCK, hd), h0),
                slot_block(),
            ],
            out_specs=[
                head_block(blk, 0),
                head_block(blk, 0),
                head_block((2,) + blk, 0),
                head_block((2, 2, BLOCK, hd), 0),
                head_block((2, 2, BLOCK, hd), 0),
                slot_block(),
            ],
            out_shape=[
                jax.ShapeDtypeStruct((hc,) + blk, BF16),
                jax.ShapeDtypeStruct((hc,) + blk, BF16),
                jax.ShapeDtypeStruct((hc, 2) + blk, F32),
                jax.ShapeDtypeStruct((hc, 2, 2, BLOCK, hd), BF16),
                jax.ShapeDtypeStruct((hc, 2, 2, BLOCK, hd), F32),
                slot_shape,
            ],
            scratch_shapes=[
                pltpu.VMEM((per_device + 2, BLOCK, hd), BF16),
                pltpu.VMEM((per_device + 2, BLOCK, hd), BF16),
                pltpu.VMEM((2, (5 + links) * BLOCK, hd), BF16),
                pltpu.VMEM((2, (5 + links) * BLOCK, hd), BF16),
                pltpu.VMEM((2, per_device + 2, BLOCK, hd), F32),
                pltpu.VMEM((2, 2, BLOCK, hd), F32),
            ],
            compiler_params=params(),
            cost_estimate=pl.CostEstimate(
                flops=10 * hc * seq_local * (5 + links) * BLOCK * hd,
                bytes_accessed=hc * (slots * 8 + per_device * 20) * BLOCK * hd,
                transcendentals=hc * seq_local * (5 + links) * BLOCK,
            ),
            name="attend",
        )(place, flags, q, g, k, v, prev_edge, next_edge, anchors, arrived[c])

    done = [attend(c) for c in range(chunks)]
    returned = [exchange(done[c][5]) for c in range(chunks)]

    def joined(n):
        parts = [done[c][n] for c in range(chunks)]
        return parts[0] if chunks == 1 else jnp.concatenate(parts, axis=0)

    edges = joined(3)
    from_prev = lax.ppermute(edges[:, 1], "ctx", up)
    from_next = lax.ppermute(edges[:, 0], "ctx", down)
    dan = joined(4)
    mine = jnp.where(lower, dan[:, 0], dan[:, 1])
    theirs = jnp.where(lower, dan[:, 1], dan[:, 0])
    total = mine + lax.ppermute(theirs, "ctx", swap)
    for bit, pairs in reversed(spread):
        total = total + lax.ppermute(total, "ctx", [(b, a) for a, b in pairs])

    def finish(c):
        h0 = c * hc
        return pl.pallas_call(
            functools.partial(
                finish_kernel,
                head0=h0,
                slots=slots,
                capacity=capacity,
                per_device=per_device,
            ),
            grid=(hc,),
            in_specs=[
                smem(),
                smem(),
                head_block((2,) + blk, 0),
                slot_block(),
                head_block((2, BLOCK, hd), h0),
                head_block((2, BLOCK, hd), h0),
                head_block((2, BLOCK, hd), h0),
            ],
            out_specs=[head_block(blk, 0), head_block(blk, 0)],
            out_shape=[jax.ShapeDtypeStruct((hc,) + blk, BF16)] * 2,
            scratch_shapes=[pltpu.VMEM((2,) + blk, F32)],
            compiler_params=params(),
            cost_estimate=pl.CostEstimate(
                flops=0,
                bytes_accessed=hc * (slots * 4 + per_device * 12) * BLOCK * hd,
                transcendentals=0,
            ),
            name="finish",
        )(wanted, flags, done[c][2], returned[c], from_prev, from_next, total)

    grads = [finish(c) for c in range(chunks)]

    def whole(parts):
        return seq_major(parts[0] if chunks == 1 else jnp.concatenate(parts, axis=0))

    return (
        whole([d[0] for d in done]),
        whole([d[1] for d in done]),
        whole([x[0] for x in grads]),
        whole([x[1] for x in grads]),
    )


def solution(mesh):
    rows = P("ctx", "head", None)
    return jax.shard_map(
        local,
        mesh=mesh,
        in_specs=(rows, rows, rows, rows, P(None, "head", None)),
        out_specs=(rows, rows, rows, rows),
        check_vma=False,
    )
```

```python
import functools
import math

import jax
import jax.numpy as jnp
from jax import lax
from jax.experimental import pallas as pl
from jax.experimental.pallas import tpu as pltpu
from jax.sharding import PartitionSpec as P

BLOCK = 64
CHUNKS = 2
F32 = jnp.float32
BF16 = jnp.bfloat16


def dot(a, b, dims):
    return lax.dot_general(a, b, (dims, ((), ())), preferred_element_type=F32)


def serve_kernel(wanted_ref, kv_ref, out_ref, *, head0, slots, capacity):
    h = head0 + pl.program_id(0)

    def body(s, carry):
        j = jnp.maximum(wanted_ref[h * slots + s], 0)
        t = s // capacity
        c = s - t * capacity
        out_ref[t, 0, c] = kv_ref[0, :, j]
        return carry

    lax.fori_loop(0, slots, body, 0, unroll=4)


def land_kernel(wanted_ref, back_ref, out_ref, acc, *, head0, slots, capacity):
    h = head0 + pl.program_id(0)
    acc[...] = jnp.zeros_like(acc)
    gather_slots(wanted_ref, back_ref, acc, h, slots, capacity)
    out_ref[0] = acc[...].astype(BF16)


def gather_slots(wanted_ref, back_ref, acc, h, slots, capacity):
    def body(s, carry):
        j = wanted_ref[h * slots + s]
        t = s // capacity
        c = s - t * capacity

        @pl.when(j >= 0)
        def _():
            acc[:, j] += back_ref[t, 0, c].astype(F32)

        return carry

    lax.fori_loop(0, slots, body, 0)


def attend_kernel(
    place_ref,
    flag_ref,
    q_ref,
    g_ref,
    kv_ref,
    prev_ref,
    next_ref,
    anchor_ref,
    arr0_ref,
    arr1_ref,
    att_ref,
    dq_ref,
    near_ref,
    edge_ref,
    dan_ref,
    send0_ref,
    send1_ref,
    kx,
    vx,
    kc,
    vc,
    accw,
    acca,
    *,
    head0,
    per_device,
    links,
    slots,
    capacity,
    scaling,
):
    h = head0 + pl.program_id(0)
    hd = q_ref.shape[-1]
    refs = per_device * links
    wide = 3 * BLOCK
    fixed = 5 * BLOCK
    total = fixed + links * BLOCK
    for dst, side in ((kx, 0), (vx, 1)):
        dst[0] = prev_ref[0, side]
        dst[1 : per_device + 1] = kv_ref[0, side]
        dst[per_device + 1] = next_ref[0, side]
    for dst, side in ((kc, 0), (vc, 1)):
        for slot in range(2):
            dst[slot, wide:fixed] = anchor_ref[0, :, side].reshape(2 * BLOCK, hd)
    accw[...] = jnp.zeros_like(accw)
    acca[...] = jnp.zeros_like(acca)
    no_prev = flag_ref[0] == 0
    no_next = flag_ref[1] == 0

    def one(i, slot):
        spots = []
        for r in range(links):
            place = place_ref[h * refs + i * links + r]
            far = place >= slots
            rest = jnp.where(far, place - slots, place)
            t = rest // capacity
            spots.append((far, t, rest - t * capacity))
        for dst, src, side in ((kc, kx, 0), (vc, vx, 1)):
            dst[slot, 0:wide] = src[pl.ds(i, 3)].reshape(wide, hd)
            for r, (far, t, c) in enumerate(spots):
                dst[slot, fixed + r * BLOCK : fixed + (r + 1) * BLOCK] = jnp.where(
                    far, arr1_ref[t, 0, c, side], arr0_ref[t, 0, c, side]
                )
        q = q_ref[0, i]
        g = g_ref[0, i]
        keys = kc[slot]
        vals = vc[slot]
        s = dot(q, keys, ((1,), (1,)))
        dp = dot(g, vals, ((1,), (1,)))
        col = lax.broadcasted_iota(jnp.int32, (BLOCK, total), 1)
        low = jnp.where(jnp.logical_and(i == 0, no_prev), BLOCK, 0)
        high = jnp.where(jnp.logical_and(i == per_device - 1, no_next), 2 * BLOCK, wide)
        hidden = (col < low) | ((col >= high) & (col < wide))
        s = jnp.where(hidden, -1e30, s)
        m = jnp.max(s, axis=1, keepdims=True)
        p = jnp.where(hidden, 0.0, jnp.exp((s - m) * scaling))
        p = p * (1.0 / jnp.sum(p, axis=1, keepdims=True))
        low_p = p.astype(BF16)
        o = dot(low_p, vals, ((1,), (0,))).astype(BF16)
        att_ref[0, i] = o
        delta = jnp.sum(g.astype(F32) * o.astype(F32), axis=1, keepdims=True)
        ds = (p * (dp - delta)).astype(BF16)
        dq_ref[0, i] = (scaling * dot(ds, keys, ((1,), (0,)))).astype(BF16)
        dk = scaling * dot(ds, q, ((0,), (0,)))
        dv = dot(low_p, g, ((0,), (0,)))
        for side, term in ((0, dk), (1, dv)):
            accw[side, pl.ds(i, 3)] += term[:wide].reshape(3, BLOCK, hd)
            acca[side] += term[wide:fixed].reshape(2, BLOCK, hd)
            for r, (far, t, c) in enumerate(spots):
                piece = term[fixed + r * BLOCK : fixed + (r + 1) * BLOCK].astype(BF16)

                @pl.when(far)
                def _():
                    send1_ref[t, 0, c, side] = piece

                @pl.when(jnp.logical_not(far))
                def _():
                    send0_ref[t, 0, c, side] = piece

    def pair(n, carry):
        one(2 * n, 0)
        one(2 * n + 1, 1)
        return carry

    lax.fori_loop(0, per_device // 2, pair, 0)
    near_ref[0] = accw[:, 1 : per_device + 1]
    edge_ref[0, 0] = accw[:, 0].astype(BF16)
    edge_ref[0, 1] = accw[:, per_device + 1].astype(BF16)
    dan_ref[0, 0] = acca[:, 0]
    dan_ref[0, 1] = acca[:, 1]


def finish_kernel(
    wanted_ref,
    flag_ref,
    near_ref,
    back_ref,
    far_ref,
    up_ref,
    down_ref,
    anchor_ref,
    dk_ref,
    dv_ref,
    acc,
    *,
    head0,
    slots,
    capacity,
    per_device,
):
    h = head0 + pl.program_id(0)
    acc[...] = near_ref[0] + far_ref[0].astype(F32)
    acc[:, 0] += up_ref[0].astype(F32)
    acc[:, per_device - 1] += down_ref[0].astype(F32)

    @pl.when(flag_ref[0] == 0)
    def _():
        acc[:, 0] += anchor_ref[0]

    @pl.when(flag_ref[1] == 0)
    def _():
        acc[:, per_device - 1] += anchor_ref[0]

    gather_slots(wanted_ref, back_ref, acc, h, slots, capacity)
    dk_ref[0] = acc[0].astype(BF16)
    dv_ref[0] = acc[1].astype(BF16)


def local(query, key, value, out_grad, random_links):
    seq_local, heads, hd = query.shape
    per_device = seq_local // BLOCK
    links = random_links.shape[2]
    ctx = lax.axis_size("ctx")
    me = lax.axis_index("ctx")
    half = ctx // 2
    side = me // half
    partner = (me + half) % ctx
    refs = per_device * links
    capacity = max(2, (5 * refs + 4 * ctx - 1) // (4 * ctx))
    slots = half * capacity
    scaling = 1.0 / math.sqrt(hd)
    chunks = CHUNKS if heads % CHUNKS == 0 else 1
    hc = heads // chunks
    halves = [list(range(half)), list(range(half, ctx))]
    swap = [(n, (n + half) % ctx) for n in range(ctx)]
    up = [(n, n + 1) for n in range(ctx - 1)]
    down = [(n + 1, n) for n in range(ctx - 1)]

    def send(array, pairs):
        return lax.ppermute(array, "ctx", pairs)

    def exchange(array):
        return lax.all_to_all(
            array, "ctx", split_axis=0, concat_axis=0, axis_index_groups=halves, tiled=True
        )

    def head_major(array):
        return array.reshape(per_device, BLOCK, heads, hd).transpose(2, 0, 1, 3)

    def seq_major(array):
        return array.transpose(1, 2, 0, 3).reshape(seq_local, heads, hd)

    kv = jnp.stack((head_major(key), head_major(value)), axis=1)
    q = head_major(query)
    g = head_major(out_grad)
    kvs = [kv[c * hc : (c + 1) * hc] for c in range(chunks)]

    def edge(start):
        rows = jnp.stack((key[start : start + BLOCK], value[start : start + BLOCK]))
        return rows.transpose(2, 0, 1, 3)

    first, last = edge(0), edge(seq_local - BLOCK)

    across = [(0, half), (ctx - 1, half - 1)]
    anchor = jnp.where(me == 0, first, last)
    moved = send(anchor, across)
    anchor = jnp.where((me == half) | (me == half - 1), moved, anchor)
    rank = me % half
    turn = half // 2
    lower = rank < turn
    rank = jnp.where(lower, rank, half - 1 - rank)
    spread = []
    known = 1
    while known < turn:
        pairs = [(n, n + known) for n in range(known)]
        pairs += [(half - 1 - a, half - 1 - b) for a, b in pairs]
        pairs += [(half + a, half + b) for a, b in pairs]
        spread.append(pairs)
        moved = send(anchor, pairs)
        anchor = jnp.where((rank >= known) & (rank < 2 * known), moved, anchor)
        known *= 2
    cross = [(n, n ^ turn) for n in range(ctx)]
    other = send(anchor, cross)
    anchors = jnp.stack(
        (jnp.where(lower, anchor, other), jnp.where(lower, other, anchor)), axis=1
    )

    swapped = [send(kvs[c], swap) for c in range(chunks)]
    prev_edge = send(last, up)
    next_edge = send(first, down)

    table = random_links.transpose(1, 0, 2).reshape(heads, ctx, refs)
    before = jnp.arange(refs)[:, None] > jnp.arange(refs)[None, :]
    asking = lax.dynamic_slice_in_dim(table, side * half, half, 1)

    def wanted_of(holder):
        aimed = (asking // per_device) == holder
        order = jnp.sum((aimed[:, :, None, :] & before).astype(jnp.int32), axis=3)
        hit = aimed[:, :, None, :] & (order[:, :, None, :] == jnp.arange(capacity)[:, None])
        found = jnp.sum(jnp.where(hit, asking[:, :, None, :] % per_device + 1, 0), axis=3)
        return (found - 1).reshape(heads * slots)

    wanted = [wanted_of(me), wanted_of(partner)]
    own = lax.dynamic_index_in_dim(table, me, 1, keepdims=False)
    owner = own // per_device
    same = (owner[:, :, None] == owner[:, None, :]) & before
    place = (owner % half) * capacity + jnp.sum(same.astype(jnp.int32), axis=2)
    place = (place + jnp.where(owner // half == side, 0, slots)).reshape(heads * refs)
    flags = jnp.stack((me > 0, me < ctx - 1)).astype(jnp.int32)

    def smem():
        return pl.BlockSpec(memory_space=pltpu.SMEM)

    def head_block(shape, head0):
        zeros = (0,) * (len(shape))
        return pl.BlockSpec((1,) + shape, lambda n: (head0 + n,) + zeros)

    def slot_block(head0):
        return pl.BlockSpec(
            (half, 1, capacity, 2, BLOCK, hd), lambda n: (0, head0 + n, 0, 0, 0, 0)
        )

    blk = (per_device, BLOCK, hd)
    pair = (2, BLOCK, hd)

    def slot_shape(count):
        return jax.ShapeDtypeStruct((half, count, capacity, 2, BLOCK, hd), BF16)

    params = pltpu.CompilerParams(dimension_semantics=("arbitrary",))

    def cost(count, flops=0, exps=0):
        return pl.CostEstimate(
            flops=flops, bytes_accessed=count * BLOCK * hd, transcendentals=exps
        )

    def serve(which, array, head0, count):
        return pl.pallas_call(
            functools.partial(serve_kernel, head0=head0, slots=slots, capacity=capacity),
            grid=(count,),
            in_specs=[smem(), head_block((2,) + blk, 0)],
            out_specs=slot_block(0),
            out_shape=slot_shape(count),
            compiler_params=params,
            cost_estimate=cost(count * (slots * 4 + per_device * 4)),
            name="serve",
        )(wanted[which], array)

    near_slots = exchange(serve(0, kv, 0, heads))
    far_slots = [exchange(serve(1, swapped[c], c * hc, hc)) for c in range(chunks)]

    def attend(c):
        h0 = c * hc
        return pl.pallas_call(
            functools.partial(
                attend_kernel,
                head0=h0,
                per_device=per_device,
                links=links,
                slots=slots,
                capacity=capacity,
                scaling=scaling,
            ),
            grid=(hc,),
            in_specs=[
                smem(),
                smem(),
                head_block(blk, h0),
                head_block(blk, h0),
                head_block((2,) + blk, h0),
                head_block(pair, h0),
                head_block(pair, h0),
                head_block((2,) + pair, h0),
                slot_block(h0),
                slot_block(0),
            ],
            out_specs=[
                head_block(blk, 0),
                head_block(blk, 0),
                head_block((2,) + blk, 0),
                head_block((2,) + pair, 0),
                head_block((2,) + pair, 0),
                slot_block(0),
                slot_block(0),
            ],
            out_shape=[
                jax.ShapeDtypeStruct((hc,) + blk, BF16),
                jax.ShapeDtypeStruct((hc,) + blk, BF16),
                jax.ShapeDtypeStruct((hc, 2) + blk, F32),
                jax.ShapeDtypeStruct((hc, 2) + pair, BF16),
                jax.ShapeDtypeStruct((hc, 2) + pair, F32),
                slot_shape(hc),
                slot_shape(hc),
            ],
            scratch_shapes=[
                pltpu.VMEM((per_device + 2, BLOCK, hd), BF16),
                pltpu.VMEM((per_device + 2, BLOCK, hd), BF16),
                pltpu.VMEM((2, (5 + links) * BLOCK, hd), BF16),
                pltpu.VMEM((2, (5 + links) * BLOCK, hd), BF16),
                pltpu.VMEM((2, per_device + 2, BLOCK, hd), F32),
                pltpu.VMEM((2, 2, BLOCK, hd), F32),
            ],
            compiler_params=params,
            cost_estimate=cost(
                hc * (slots * 16 + per_device * 20),
                10 * hc * seq_local * (5 + links) * BLOCK * hd,
                hc * seq_local * (5 + links) * BLOCK,
            ),
            name="attend",
        )(place, flags, q, g, kv, prev_edge, next_edge, anchors, near_slots, far_slots[c])

    done = [attend(c) for c in range(chunks)]

    def land(c):
        return pl.pallas_call(
            functools.partial(land_kernel, head0=c * hc, slots=slots, capacity=capacity),
            grid=(hc,),
            in_specs=[smem(), slot_block(0)],
            out_specs=head_block((2,) + blk, 0),
            out_shape=jax.ShapeDtypeStruct((hc, 2) + blk, BF16),
            scratch_shapes=[pltpu.VMEM((2,) + blk, F32)],
            compiler_params=params,
            cost_estimate=cost(hc * (slots * 4 + per_device * 4)),
            name="land",
        )(wanted[1], exchange(done[c][6]))

    from_partner = [send(land(c), swap) for c in range(chunks)]
    returned = [exchange(done[c][5]) for c in range(chunks)]

    def joined(parts):
        return parts[0] if chunks == 1 else jnp.concatenate(parts, axis=0)

    edges = joined([d[3] for d in done])
    from_prev = send(edges[:, 1], up)
    from_next = send(edges[:, 0], down)
    dan = joined([d[4] for d in done])
    mine = jnp.where(lower, dan[:, 0], dan[:, 1])
    theirs = jnp.where(lower, dan[:, 1], dan[:, 0])
    total = mine + send(theirs, cross)
    for pairs in reversed(spread):
        total = total + send(total, [(b, a) for a, b in pairs])
    total = total + send(total, [(b, a) for a, b in across])

    def finish(c):
        h0 = c * hc
        return pl.pallas_call(
            functools.partial(
                finish_kernel,
                head0=h0,
                slots=slots,
                capacity=capacity,
                per_device=per_device,
            ),
            grid=(hc,),
            in_specs=[
                smem(),
                smem(),
                head_block((2,) + blk, 0),
                slot_block(0),
                head_block((2,) + blk, 0),
                head_block(pair, h0),
                head_block(pair, h0),
                head_block(pair, h0),
            ],
            out_specs=[head_block(blk, 0), head_block(blk, 0)],
            out_shape=[jax.ShapeDtypeStruct((hc,) + blk, BF16)] * 2,
            scratch_shapes=[pltpu.VMEM((2,) + blk, F32)],
            compiler_params=params,
            cost_estimate=cost(hc * (slots * 4 + per_device * 16)),
            name="finish",
        )(
            wanted[0],
            flags,
            done[c][2],
            returned[c],
            from_partner[c],
            from_prev,
            from_next,
            total,
        )

    grads = [finish(c) for c in range(chunks)]

    return (
        seq_major(joined([d[0] for d in done])),
        seq_major(joined([d[1] for d in done])),
        seq_major(joined([x[0] for x in grads])),
        seq_major(joined([x[1] for x in grads])),
    )


def solution(mesh):
    rows = P("ctx", "head", None)
    return jax.shard_map(
        local,
        mesh=mesh,
        in_specs=(rows, rows, rows, rows, P(None, "head", None)),
        out_specs=(rows, rows, rows, rows),
        check_vma=False,
    )
```
